256 devices in a mesh: section: 4 (over y_lo, core), dp: 64 (over z, x, y_hi).
Axes of the slice: x: 4, y: 4 (y_hi: 2, y_lo: 2; y = y_hi * 2 + y_lo), z: 8, core: 2. Of those that a mesh axis runs over, the one named last changes fastest.
Arguments:
- replay: bfloat16 [8192, 4096], P('dp'), may hold values from -6 to 6
- state_ids: int32 [8192], P('dp'), may hold values from 0 to 8191, as said below
- sampled: int32 [8192, 20], P('dp'), may hold values from 0 to 255
- targets: int32 [8192], P('dp'), may hold values from 0 to 19
- action_table: bfloat16 [256, 4096], replicated, may hold values from -6 to 6
- norm_gain: float32 [4, 4096], P('section'), may hold values from 0.5 to 1.5
- w_up: bfloat16 [4, 4096, 512], P('section', 'dp'), may hold values from -0.09375 to 0.09375
- w_down: bfloat16 [4, 512, 4096], P('section', 'dp'), may hold values from -0.25 to 0.25
Outputs:
- grad_up: float32 [4, 4096, 512], P('section', 'dp')
- grad_down: float32 [4, 512, 4096], P('section', 'dp')
- grad_gain: float32 [4, 4096], P('section')
- loss: float32 [], replicated
The draws below stay inside these ranges and needn't reach their ends.
Inputs may be any that keep to these rules, and one draw needn't show every extreme that they name: state_ids[i] // 128 == i // 128: a state's replay row lies in the same aligned block of 128 rows as the state.
All inputs are finite; a program needn't handle non-finite values.
Results may differ from the reference program's by a relative error of at most 0.011.
Values may be sent and summed in bfloat16 or wider, within the bound.
No kernel may reach another device: no remote copies, remote signals or barrier semaphores. Data moves between devices by JAX's collectives and lax.ppermute only.
A program may use at most 128 MiB of HBM per device.

```python
import math
import jax
import jax.numpy as jnp
from jax import lax

D = 4096
FF = 512
VOCAB = 256
SAMPLES = 20
ROWS_DEV = 128
ROWS = 8192
N_LAYERS = 4


def draw_state_ids(key, part):
    offset = jnp.arange(ROWS) // ROWS_DEV * ROWS_DEV
    return (jax.random.randint(key, (ROWS,), 0, ROWS_DEV) + offset).astype(jnp.int32)


def with_ends(entries, key, low, top_value):
    longest = entries.shape.index(max(entries.shape))
    spots = []
    for shift in (0, 1):
        where = [jax.random.randint(jax.random.fold_in(key, axis), (), 0, length) for axis, length in enumerate(entries.shape)]
        where[longest] = (where[longest] + shift) % entries.shape[longest]
        spots.append(tuple(where))
    return entries.at[spots[0]].set(low).at[spots[1]].set(top_value)


def steps_of(rng, shape, cuts, low, high):
    loudness = 1.0
    for dim, blocks in cuts:
        heights = jax.random.uniform(jax.random.fold_in(jax.random.fold_in(rng, 6), dim), (blocks,), jnp.float32, low / len(cuts), high / len(cuts))
        loudness = loudness * jnp.repeat(jnp.exp(heights), shape[dim] // blocks).reshape((-1,) + (1,) * (len(shape) - 1 - dim))
    return loudness


def bell_draw(rng, dims, deviation, limit, shards=(), kind=jnp.bfloat16):
    values = deviation * jax.random.normal(rng, dims, jnp.float32)
    if shards:
        values = values * steps_of(rng, dims, shards, -0.22, 0.18)
    return jnp.clip(values, -limit, limit).astype(kind)


def setup_inputs(seed: int = 0) -> dict:
    arg_keys = jax.random.split(jax.random.key(seed), 9)
    return {
        "replay": bell_draw(arg_keys[0], (ROWS, D), 1.0, 6.0, ((0, 64),)),
        "state_ids": draw_state_ids(jax.random.fold_in(arg_keys[8], 71), 0),
        "sampled": with_ends(jax.random.randint(arg_keys[2], (ROWS, SAMPLES), 0, VOCAB), jax.random.fold_in(arg_keys[2], 1), 0, VOCAB - 1).astype(jnp.int32),
        "targets": with_ends(jax.random.randint(arg_keys[3], (ROWS,), 0, SAMPLES), jax.random.fold_in(arg_keys[3], 1), 0, SAMPLES - 1).astype(jnp.int32),
        "action_table": bell_draw(arg_keys[4], (VOCAB, D), 1.0, 6.0),
        "norm_gain": jnp.clip(1.0 + 0.1 * jax.random.normal(arg_keys[5], (N_LAYERS, D), jnp.float32), 0.5, 1.5),
        "w_up": bell_draw(arg_keys[6], (N_LAYERS, D, FF), D ** -0.5, 0.09375, ((0, 4), (1, 64))),
        "w_down": bell_draw(arg_keys[7], (N_LAYERS, FF, D), FF ** -0.5, 0.25, ((0, 4), (1, 64))),
    }


epsilon = 1e-06
logit_cap = 15.0

def contract_last(left, right):
    return lax.dot_general(left, right, (((1,), (1,)), ((), ())), preferred_element_type=jnp.float32)

def contract_first(left, right):
    return lax.dot_general(left, right, (((0,), (0,)), ((), ())), preferred_element_type=jnp.float32)

def layer_forward(states, gain_row, up_proj, down_proj):
    wide = states.astype(jnp.float32)
    recip = lax.rsqrt(lax.optimization_barrier(jnp.mean(wide * wide, -1, keepdims=True)) + epsilon)
    normed = (wide * recip * gain_row).astype(jnp.bfloat16)
    upper = jnp.dot(normed, up_proj, preferred_element_type=jnp.float32)
    sigm = jax.nn.sigmoid(upper)
    active = (upper * sigm).astype(jnp.bfloat16)
    result = (wide + jnp.dot(active, down_proj, preferred_element_type=jnp.float32)).astype(jnp.bfloat16)
    return (result, (wide, recip, normed, upper, sigm, active))

def layer_backward(grad_out, cache, gain_row, up_proj, down_proj):
    wide, recip, normed, upper, sigm, active = cache
    grad_act = contract_last(grad_out, down_proj)
    grad_upper = (grad_act * sigm * (1.0 + upper * (1.0 - sigm))).astype(jnp.bfloat16)
    grad_norm = contract_last(grad_upper, up_proj)
    scaled = grad_norm * gain_row
    gain_term = lax.optimization_barrier(jnp.sum(grad_norm * wide * recip, 0))
    grad_in = grad_out.astype(jnp.float32) + scaled * recip - wide * recip ** 3 * lax.optimization_barrier(jnp.mean(scaled * wide, -1, keepdims=True))
    return (grad_in.astype(jnp.bfloat16), grad_upper, gain_term)

def head_tail(chosen, targets, scale):
    bent = jnp.tanh(chosen / logit_cap)
    logits = logit_cap * bent
    expo = jnp.exp(logits)
    summed = lax.optimization_barrier(jnp.sum(expo, -1, keepdims=True))
    target_hot = (targets[:, None] == jnp.arange(chosen.shape[1])[None, :]).astype(jnp.float32)
    cross = jnp.log(summed[:, 0]) - lax.optimization_barrier(jnp.sum(logits * target_hot, -1))
    loss_sum = jnp.sum(cross) / ROWS_DEV
    d_logits = (expo / summed - target_hot) / ROWS_DEV
    d_chosen = d_logits * (1.0 - bent * bent) / scale
    return (loss_sum, d_chosen)

def reference(replay, state_ids, sampled, targets, action_table, norm_gain, w_up, w_down):
    picked = jnp.take(replay, state_ids, axis=0)
    embedded = jnp.take(action_table, sampled[:, 0], axis=0)
    hidden = (picked.astype(jnp.float32) + embedded.astype(jnp.float32)).astype(jnp.bfloat16)
    kept_inputs = []
    for layer_idx in range(N_LAYERS):
        kept_inputs.append(hidden)
        hidden, _ = layer_forward(hidden, norm_gain[layer_idx], w_up[layer_idx], w_down[layer_idx])
    scale = math.sqrt(D)
    scores = contract_last(hidden, action_table) / scale
    chosen = jnp.take_along_axis(scores, sampled, axis=1)
    loss_sum, d_chosen = head_tail(chosen, targets, scale)
    row_ids = jnp.arange(scores.shape[0])[:, None]
    d_scores = jnp.zeros(scores.shape, jnp.float32).at[row_ids, sampled].add(d_chosen)
    grad_state = jnp.dot(d_scores.astype(jnp.bfloat16), action_table, preferred_element_type=jnp.float32).astype(jnp.bfloat16)
    ups, downs, gains = ([], [], [])
    for layer_idx in reversed(range(N_LAYERS)):
        _, cache = layer_forward(kept_inputs[layer_idx], norm_gain[layer_idx], w_up[layer_idx], w_down[layer_idx])
        downs.append(contract_first(cache[5], grad_state))
        grad_state_new, grad_upper, gain_term = layer_backward(grad_state, cache, norm_gain[layer_idx], w_up[layer_idx], w_down[layer_idx])
        ups.append(contract_first(cache[2], grad_upper))
        gains.append(gain_term)
        grad_state = grad_state_new
    return (jnp.stack(ups[::-1]), jnp.stack(downs[::-1]), jnp.stack(gains[::-1]), loss_sum)
```

```python
import math

import jax
import jax.numpy as jnp
from jax import lax
from jax.sharding import Mesh, PartitionSpec as P

ROWS_DEV = 128
SECTIONS = 4
GATHER_GROUPS = ((0, 1), (2, 3))
SCATTER_GROUPS = ((3, 2), (1, 0))

epsilon = 1e-06
logit_cap = 15.0
f32 = jnp.float32
bf16 = jnp.bfloat16
GROUP = ("yl", "core")


def matmul(left, right, dims):
    return lax.dot_general(left, right, (dims, ((), ())), preferred_element_type=f32)


def shift(value, axis, by):
    n = lax.axis_size(axis)
    return lax.ppermute(value, axis, [(i, (i + by) % n) for i in range(n)])


def swap(value, axis, mask):
    n = lax.axis_size(axis)
    return lax.ppermute(value, axis, [(i, i ^ mask) for i in range(n)])


def halves(value, dim):
    mid = value.shape[dim] // 2
    return (
        lax.slice_in_dim(value, 0, mid, axis=dim),
        lax.slice_in_dim(value, mid, value.shape[dim], axis=dim),
    )


def ring_gather(block, axis, dim, split):
    n, me = lax.axis_size(axis), lax.axis_index(axis)
    shape = block.shape[:dim] + (n,) + block.shape[dim:]
    whole = jnp.zeros(shape, block.dtype)
    at_split = split + 1 if split >= dim else split

    def placed(buffer, value, member, offset=0):
        start = [0] * len(shape)
        start[dim] = member % n
        start[at_split] = offset
        return lax.dynamic_update_slice(buffer, jnp.expand_dims(value, dim), start)

    whole = placed(whole, block, me)
    up = down = block
    for step in range(1, n // 2):
        up, down = shift(up, axis, 1), shift(down, axis, -1)
        whole = placed(whole, up, me - step + n)
        whole = placed(whole, down, me + step)
    up = shift(halves(up, split)[0], axis, 1)
    down = shift(halves(down, split)[1], axis, -1)
    whole = placed(whole, up, me + n // 2)
    return placed(whole, down, me + n // 2, block.shape[split] // 2)


def ring_scatter(parts, axis, dim, split):
    n, me = lax.axis_size(axis), lax.axis_index(axis)

    def part(offset):
        return lax.dynamic_index_in_dim(parts, (me + offset + n) % n, dim, keepdims=False)

    up, down = halves(part(n // 2), split)
    up, down = shift(up, axis, 1), shift(down, axis, -1)
    for step in range(n // 2 - 1, 0, -1):
        first, second = part(step).astype(f32), part(-step).astype(f32)
        if step == n // 2 - 1:
            low, high = halves(first, split)
            first = jnp.concatenate([low + up.astype(f32), high], split)
            low, high = halves(second, split)
            second = jnp.concatenate([low, high + down.astype(f32)], split)
        else:
            first, second = first + up.astype(f32), second + down.astype(f32)
        up, down = shift(first.astype(bf16), axis, 1), shift(second.astype(bf16), axis, -1)
    return part(0).astype(f32) + up.astype(f32) + down.astype(f32)


def group_sum(value):
    kind = value.dtype
    first = value.astype(f32) + swap(value, GROUP, 1).astype(f32)
    first = first.astype(kind)
    return first.astype(f32) + swap(first, GROUP, 2).astype(f32)


def group_exchange(blocks, me):
    def block(member):
        return lax.dynamic_index_in_dim(blocks, member, 0, keepdims=False)

    got = [block(me)] + [swap(block(me ^ mask), GROUP, mask) for mask in range(1, SECTIONS)]
    got = jnp.stack(got)
    return jnp.stack(
        [lax.dynamic_index_in_dim(got, me ^ t, 0, keepdims=False) for t in range(SECTIONS)]
    )


def spread(wide, picks):
    rows, width = wide.shape
    spans = width // 512
    out = [matmul(wide[:, 512 * i : 512 * (i + 1)], picks, ((1,), (0,))) for i in range(spans)]
    return out


def head_tail(chosen, targets, scale):
    bent = jnp.tanh(chosen / logit_cap)
    logits = logit_cap * bent
    expo = jnp.exp(logits)
    summed = jnp.sum(expo, -1, keepdims=True)
    target_hot = (targets[:, None] == jnp.arange(chosen.shape[1])[None, :]).astype(f32)
    cross = jnp.log(summed[:, 0]) - jnp.sum(logits * target_hot, -1)
    loss_sum = jnp.sum(cross) / ROWS_DEV
    d_logits = (expo / summed - target_hot) / ROWS_DEV
    d_chosen = d_logits * (1.0 - bent * bent) / scale
    return (loss_sum, d_chosen)


def on_device(replay, state_ids, sampled, targets, action_table, norm_gain, w_up, w_down):
    me = lax.axis_index(GROUP)
    pos_z, pos_x, pos_yh = (lax.axis_index(a) for a in ("z", "x", "yh"))
    n_z, n_x, n_yh = (lax.axis_size(a) for a in ("z", "x", "yh"))
    dp = (pos_z * n_x + pos_x) * n_yh + pos_yh
    rows, width = replay.shape
    vocab = action_table.shape[0]
    ff = w_up.shape[2]
    quarter = width // SECTIONS
    span = quarter // n_z
    run = span // (n_x * n_yh)
    ff_rows = w_down.shape[1]

    col_in = lax.broadcasted_iota(jnp.int32, (SECTIONS * span, SECTIONS * span), 0)
    col_out = lax.broadcasted_iota(jnp.int32, (SECTIONS * span, SECTIONS * span), 1)
    t, o = col_out // span, col_out % span
    deal = (col_in == (o // run) * (run * SECTIONS) + t * run + o % run).astype(bf16)
    row_mine = lax.broadcasted_iota(jnp.int32, (SECTIONS * span, span), 0)
    o = lax.broadcasted_iota(jnp.int32, (SECTIONS * span, span), 1)
    mine = (row_mine == (o // run) * (run * SECTIONS) + me * run + o % run).astype(bf16)

    gain_col = lax.dynamic_slice_in_dim(norm_gain[0], dp * run * SECTIONS, run * SECTIONS)[:, None]
    scaled_up = (w_up[0].astype(f32) * gain_col).astype(bf16)
    up_cut = scaled_up.reshape(SECTIONS, run, ff)
    dealt = [b.astype(bf16).reshape(ff_rows, SECTIONS, span) for b in spread(w_down[0], deal)]
    down_cut = jnp.stack(dealt, 2).transpose(1, 0, 2, 3)
    down_cut = down_cut.reshape(SECTIONS, run, ff)
    layers = group_exchange(jnp.concatenate([up_cut, down_cut], 1), me)

    other = swap(layers, "yh", 1)
    is_low = pos_yh == 0
    pair = jnp.stack([jnp.where(is_low, layers, other), jnp.where(is_low, other, layers)], 1)
    up_small = pair[:, :, :run].reshape(SECTIONS, n_yh * run, ff)
    down_small = pair[:, :, run:].reshape(SECTIONS, n_yh * ff_rows, quarter)

    up_small = ring_gather(up_small, "x", 1, 1).reshape(SECTIONS, span, ff)
    down_small = ring_gather(down_small, "z", 1, 2)
    up_full, down_full = {}, {}
    for group in GATHER_GROUPS:
        lo, hi = min(group), max(group) + 1
        ups = ring_gather(up_small[lo:hi], "z", 1, 1)
        downs = ring_gather(down_small[lo:hi], "x", 2, 1)
        for l in range(lo, hi):
            up_full[l] = ups[l - lo].reshape(quarter, ff)
            down_full[l] = downs[l - lo].reshape(ff, quarter)

    both = jnp.concatenate([replay, action_table], 0)
    both = jnp.concatenate([b.astype(bf16) for b in spread(both, mine)], 1)
    table = both[rows:]
    local_ids = state_ids - dp * rows
    choices = jnp.arange(rows + vocab)[None, :]
    hot = (local_ids[:, None] == choices) | (sampled[:, 0:1] + rows == choices)
    state = matmul(hot.astype(bf16), both, ((1,), (0,))).astype(bf16)

    kept = []
    for l in range(SECTIONS):
        wide = state.astype(f32)
        square = jnp.sum(wide * wide, -1, keepdims=True)
        coarse = square.astype(bf16)
        fine = (square - coarse.astype(f32)).astype(bf16)
        lane = lax.broadcasted_iota(jnp.int32, (rows, 128), 1)
        extra = jnp.where(lane == 0, coarse, jnp.where(lane == 1, fine, jnp.zeros_like(fine)))
        part = matmul(state, up_full[l], ((1,), (0,)))
        total = group_sum(jnp.concatenate([part.astype(bf16), extra], 1))
        raw = total[:, :ff]
        square = total[:, ff : ff + 1] + total[:, ff + 1 : ff + 2]
        recip = lax.rsqrt(square / width + epsilon)
        upper = raw * recip
        sigm = jax.nn.sigmoid(upper)
        active = (upper * sigm).astype(bf16)
        kept.append((state, recip, raw, upper, sigm, active))
        state = (wide + matmul(active, down_full[l], ((1,), (0,)))).astype(bf16)

    scale = math.sqrt(width)
    scores = group_sum(matmul(state, table, ((1,), (1,)))) / scale
    action_hot = (sampled[:, :, None] == jnp.arange(vocab)[None, None, :]).astype(f32)
    chosen = jnp.einsum("ra,rka->rk", scores, action_hot, precision=lax.Precision.HIGHEST)
    loss_sum, d_chosen = head_tail(chosen, targets, scale)
    d_scores = jnp.einsum(
        "rk,rka->ra", d_chosen, action_hot, precision=lax.Precision.HIGHEST
    ).astype(bf16)
    grad = matmul(d_scores, table, ((1,), (0,))).astype(bf16)

    gain_rows = [None] * SECTIONS
    up_sums, down_sums = [None] * SECTIONS, [None] * SECTIONS
    for group in SCATTER_GROUPS:
        ups, downs = {}, {}
        for l in group:
            state, recip, raw, upper, sigm, active = kept[l]
            wide = state.astype(f32)
            d_active = group_sum(matmul(grad, down_full[l], ((1,), (1,))).astype(bf16))
            downs[l] = matmul(active, grad, ((0,), (0,))).astype(bf16)
            d_raw = (d_active * sigm * (1.0 + upper * (1.0 - sigm)) * recip).astype(bf16)
            ups[l] = matmul(state, d_raw, ((0,), (0,))).astype(bf16)
            mean = jnp.sum(d_raw.astype(f32) * raw, -1, keepdims=True) / width
            through = matmul(d_raw, up_full[l], ((1,), (1,)))
            gain_rows[l] = jnp.sum(through * wide, 0)
            grad = (grad.astype(f32) + through - wide * (recip * recip * mean)).astype(bf16)
        order = sorted(group)
        up_parts = jnp.stack([ups[l].reshape(n_z, span, ff) for l in order])
        down_parts = jnp.stack(
            [downs[l].reshape(n_z, n_x, n_yh * ff_rows, quarter) for l in order]
        )
        up_parts = ring_scatter(up_parts, "z", 1, 1).astype(bf16)
        down_parts = ring_scatter(down_parts, "x", 2, 1).astype(bf16)
        for i, l in enumerate(order):
            up_sums[l] = up_parts[i]
            down_sums[l] = down_parts[i]

    gains = group_exchange(jnp.stack(gain_rows).reshape(SECTIONS, 8, quarter // 8), me)
    loss_tile = jnp.full((1, 8, quarter // 8), loss_sum)
    sums = jnp.concatenate([gains, loss_tile], 0)
    for axis in ("yh", "x", "z"):
        mask = 1
        while mask < lax.axis_size(axis):
            sums = sums + swap(sums, axis, mask)
            mask *= 2
    loss_total = sums[SECTIONS, 0, 0]
    gain_total = sums[:SECTIONS].reshape(SECTIONS, width // (run * SECTIONS), run)
    gain_total = gain_total.transpose(1, 0, 2).reshape(width) / norm_gain[0]

    up_sum = jnp.stack(up_sums).reshape(SECTIONS, n_x, n_yh * run, ff)
    up_sum = ring_scatter(up_sum, "x", 1, 1)
    down_sum = ring_scatter(jnp.stack(down_sums), "z", 1, 2)
    up_sum = up_sum.reshape(SECTIONS, n_yh, run, ff)
    down_sum = down_sum.reshape(SECTIONS, n_yh, run, ff)
    both = jnp.concatenate([up_sum, down_sum], 2)
    low, high = both[:, 0], both[:, 1]
    keep, send = jnp.where(is_low, low, high), jnp.where(is_low, high, low).astype(bf16)
    both = (keep + swap(send, "yh", 1).astype(f32)).astype(bf16)
    both = group_exchange(both, me)
    grad_up = both[:, :run].reshape(SECTIONS * run, ff).astype(f32) * gain_col
    down = both[:, run:].reshape(SECTIONS, ff_rows, n_z, span)
    spans = [
        matmul(
            down[:, :, i].transpose(1, 0, 2).reshape(ff_rows, SECTIONS * span), deal, ((1,), (1,))
        )
        for i in range(n_z)
    ]
    grad_down = jnp.concatenate(spans, 1)
    return (grad_up[None], grad_down[None], gain_total[None], loss_total)


def solution(mesh):
    sizes = (2, 2, mesh.shape["dp"] // 8, 4, 2)
    fine = Mesh(mesh.devices.reshape(sizes), ("yl", "core", "z", "x", "yh"))
    section, dp = ("yl", "core"), ("z", "x", "yh")
    return jax.shard_map(
        on_device,
        mesh=fine,
        in_specs=(
            P(dp, None),
            P(dp),
            P(dp, None),
            P(dp),
            P(),
            P(section, None),
            P(section, dp, None),
            P(section, dp, None),
        ),
        out_specs=(P(section, dp, None), P(section, dp, None), P(section, None), P()),
        check_vma=False,
    )
```

```python
import math

import jax
import jax.numpy as jnp
from jax import lax
from jax.sharding import Mesh, PartitionSpec as P

ROWS_DEV = 128
SECTIONS = 4
X_FIRST = (0, 2)

epsilon = 1e-06
logit_cap = 15.0
f32 = jnp.float32
bf16 = jnp.bfloat16
GROUP = ("yl", "core")


def matmul(left, right, dims):
    return lax.dot_general(left, right, (dims, ((), ())), preferred_element_type=f32)


def shift(value, axis, by):
    n = lax.axis_size(axis)
    return lax.ppermute(value, axis, [(i, (i + by) % n) for i in range(n)])


def swap(value, axis, mask):
    n = lax.axis_size(axis)
    return lax.ppermute(value, axis, [(i, i ^ mask) for i in range(n)])


def halves(value, dim):
    mid = value.shape[dim] // 2
    return (
        lax.slice_in_dim(value, 0, mid, axis=dim),
        lax.slice_in_dim(value, mid, value.shape[dim], axis=dim),
    )


def tied(value, after):
    return lax.optimization_barrier((value, tuple(after)))[0] if after else value


def ring_gather(block, axis, dim, split, after=()):
    block = tied(block, after)
    n, me = lax.axis_size(axis), lax.axis_index(axis)
    shape = block.shape[:dim] + (n,) + block.shape[dim:]
    whole = jnp.zeros(shape, block.dtype)
    at_split = split + 1 if split >= dim else split

    def placed(buffer, value, member, offset=0):
        start = [0] * len(shape)
        start[dim] = member % n
        start[at_split] = offset
        return lax.dynamic_update_slice(buffer, jnp.expand_dims(value, dim), start)

    whole = placed(whole, block, me)
    up = down = block
    for step in range(1, n // 2):
        up, down = shift(up, axis, 1), shift(down, axis, -1)
        whole = placed(whole, up, me - step + n)
        whole = placed(whole, down, me + step)
    up = shift(halves(up, split)[0], axis, 1)
    down = shift(halves(down, split)[1], axis, -1)
    whole = placed(whole, up, me + n // 2)
    return placed(whole, down, me + n // 2, block.shape[split] // 2), (up, down)


def ring_scatter(parts, axis, dim, split, after=()):
    n, me = lax.axis_size(axis), lax.axis_index(axis)

    def part(offset):
        return lax.dynamic_index_in_dim(parts, (me + offset + n) % n, dim, keepdims=False)

    up, down = halves(tied(part(n // 2), after), split)
    up, down = shift(up, axis, 1), shift(down, axis, -1)
    for step in range(n // 2 - 1, 0, -1):
        first, second = part(step).astype(f32), part(-step).astype(f32)
        if step == n // 2 - 1:
            low, high = halves(first, split)
            first = jnp.concatenate([low + up.astype(f32), high], split)
            low, high = halves(second, split)
            second = jnp.concatenate([low, high + down.astype(f32)], split)
        else:
            first, second = first + up.astype(f32), second + down.astype(f32)
        up, down = shift(first.astype(bf16), axis, 1), shift(second.astype(bf16), axis, -1)
    return part(0).astype(f32) + up.astype(f32) + down.astype(f32), (up, down)


def group_sum(value):
    kind = value.dtype
    first = value.astype(f32) + swap(value, GROUP, 1).astype(f32)
    first = first.astype(kind)
    return first.astype(f32) + swap(first, GROUP, 2).astype(f32)


def group_exchange(blocks, me):
    def block(member):
        return lax.dynamic_index_in_dim(blocks, member, 0, keepdims=False)

    got = [block(me)] + [swap(block(me ^ mask), GROUP, mask) for mask in range(1, SECTIONS)]
    got = jnp.stack(got)
    return jnp.stack(
        [lax.dynamic_index_in_dim(got, me ^ t, 0, keepdims=False) for t in range(SECTIONS)]
    )


def head_tail(chosen, targets, scale):
    bent = jnp.tanh(chosen / logit_cap)
    logits = logit_cap * bent
    expo = jnp.exp(logits)
    summed = jnp.sum(expo, -1, keepdims=True)
    target_hot = (targets[:, None] == jnp.arange(chosen.shape[1])[None, :]).astype(f32)
    cross = jnp.log(summed[:, 0]) - jnp.sum(logits * target_hot, -1)
    loss_sum = jnp.sum(cross) / ROWS_DEV
    d_logits = (expo / summed - target_hot) / ROWS_DEV
    d_chosen = d_logits * (1.0 - bent * bent) / scale
    return (loss_sum, d_chosen)


def on_device(replay, state_ids, sampled, targets, action_table, norm_gain, w_up, w_down):
    me = lax.axis_index(GROUP)
    pos_z, pos_x, pos_yh = (lax.axis_index(a) for a in ("z", "x", "yh"))
    n_z, n_x, n_yh = (lax.axis_size(a) for a in ("z", "x", "yh"))
    dp = (pos_z * n_x + pos_x) * n_yh + pos_yh
    rows, width = replay.shape
    vocab = action_table.shape[0]
    ff = w_up.shape[2]
    quarter = width // SECTIONS
    span = quarter // n_z
    run = span // (n_x * n_yh)
    ff_rows = w_down.shape[1]

    col_in = lax.broadcasted_iota(jnp.int32, (SECTIONS * span, SECTIONS * span), 0)
    col_out = lax.broadcasted_iota(jnp.int32, (SECTIONS * span, SECTIONS * span), 1)
    t, o = col_out // span, col_out % span
    deal = (col_in == (o // run) * (run * SECTIONS) + t * run + o % run).astype(bf16)
    row_mine = lax.broadcasted_iota(jnp.int32, (SECTIONS * span, span), 0)
    o = lax.broadcasted_iota(jnp.int32, (SECTIONS * span, span), 1)
    mine = (row_mine == (o // run) * (run * SECTIONS) + me * run + o % run).astype(bf16)

    gain_col = lax.dynamic_slice_in_dim(norm_gain[0], dp * run * SECTIONS, run * SECTIONS)[:, None]
    scaled_up = (w_up[0].astype(f32) * gain_col).astype(bf16)
    up_cut = scaled_up.reshape(SECTIONS, run, ff)
    down_cut = w_down[0].reshape(ff_rows * n_z, SECTIONS * span)
    down_cut = matmul(down_cut, deal, ((1,), (0,))).astype(bf16)
    down_cut = down_cut.reshape(ff_rows, 2, n_z // 2, SECTIONS, span).transpose(3, 1, 0, 2, 4)
    down_cut = down_cut.reshape(SECTIONS, run, ff)
    layers = group_exchange(jnp.concatenate([up_cut, down_cut], 1), me)

    other = swap(layers, "yh", 1)
    is_low = pos_yh == 0
    pair = jnp.stack([jnp.where(is_low, layers, other), jnp.where(is_low, other, layers)], 1)
    ups = pair[:, :, :run].reshape(SECTIONS, n_yh * run, ff)
    downs = pair[:, :, run:].reshape(SECTIONS, n_yh, 2, ff_rows, ff).transpose(0, 2, 1, 3, 4)
    packed = jnp.stack([ups, downs.reshape(SECTIONS, n_yh * run, ff)], 1)
    late = [l for l in range(SECTIONS) if l not in X_FIRST]
    small_x, x_done = ring_gather(jnp.stack([packed[l] for l in X_FIRST]), "x", 2, 1)
    small_z, z_done = ring_gather(jnp.stack([packed[l] for l in late]), "z", 2, 1)
    x_done, z_done = x_done + z_done, x_done
    up_full, down_full = {}, {}
    for l in range(SECTIONS):
        if l in X_FIRST:
            both, z_done = ring_gather(small_x[X_FIRST.index(l)], "z", 1, 0, z_done)
        else:
            both, x_done = ring_gather(small_z[late.index(l)], "x", 2, 0, x_done)
        up_full[l] = both[0].reshape(quarter, ff)
        down = both[1].reshape(n_z, n_x, 2, n_yh * ff_rows, ff).transpose(0, 1, 3, 2, 4)
        down_full[l] = down.reshape(ff, quarter)

    both = tied(jnp.concatenate([replay, action_table], 0), (other,))
    picked = [
        matmul(both[:, i : i + SECTIONS * span], mine, ((1,), (0,))).astype(bf16)
        for i in range(0, width, SECTIONS * span)
    ]
    both = jnp.concatenate(picked, 1)
    table = both[rows:]
    local_ids = state_ids - dp * rows
    choices = jnp.arange(rows + vocab)[None, :]
    hot = (local_ids[:, None] == choices) | (sampled[:, 0:1] + rows == choices)
    state = matmul(hot.astype(bf16), both, ((1,), (0,))).astype(bf16)

    kept = []
    for l in range(SECTIONS):
        wide = state.astype(f32)
        square = jnp.sum(wide * wide, -1, keepdims=True)
        coarse = square.astype(bf16)
        fine = (square - coarse.astype(f32)).astype(bf16)
        lane = lax.broadcasted_iota(jnp.int32, (rows, 128), 1)
        extra = jnp.where(lane == 0, coarse, jnp.where(lane == 1, fine, jnp.zeros_like(fine)))
        part = matmul(state, up_full[l], ((1,), (0,)))
        total = group_sum(jnp.concatenate([part.astype(bf16), extra], 1))
        raw = total[:, :ff]
        square = total[:, ff : ff + 1] + total[:, ff + 1 : ff + 2]
        recip = lax.rsqrt(square / width + epsilon)
        upper = raw * recip
        sigm = jax.nn.sigmoid(upper)
        active = (upper * sigm).astype(bf16)
        kept.append((state, recip, raw, upper, sigm, active))
        state = (wide + matmul(active, down_full[l], ((1,), (0,)))).astype(bf16)

    scale = math.sqrt(width)
    scores = group_sum(matmul(state, table, ((1,), (1,)))) / scale
    action_hot = (sampled[:, :, None] == jnp.arange(vocab)[None, None, :]).astype(f32)
    chosen = jnp.einsum("ra,rka->rk", scores, action_hot, precision=lax.Precision.HIGHEST)
    loss_sum, d_chosen = head_tail(chosen, targets, scale)
    d_scores = jnp.einsum(
        "rk,rka->ra", d_chosen, action_hot, precision=lax.Precision.HIGHEST
    ).astype(bf16)
    grad = matmul(d_scores, table, ((1,), (0,))).astype(bf16)

    gain_rows = [None] * SECTIONS
    small = {}
    z_done = x_done = ()
    for l in reversed(range(SECTIONS)):
        state, recip, raw, upper, sigm, active = kept[l]
        wide = state.astype(f32)
        d_active = group_sum(matmul(grad, down_full[l], ((1,), (1,))).astype(bf16))
        down = matmul(active, grad, ((0,), (0,))).astype(bf16)
        d_raw = (d_active * sigm * (1.0 + upper * (1.0 - sigm)) * recip).astype(bf16)
        up = matmul(state, d_raw, ((0,), (0,))).astype(bf16)
        mean = jnp.sum(d_raw.astype(f32) * raw, -1, keepdims=True) / width
        through = matmul(d_raw, up_full[l], ((1,), (1,)))
        gain_rows[l] = jnp.sum(through * wide, 0)
        grad = (grad.astype(f32) + through - wide * (recip * recip * mean)).astype(bf16)
        down = down.reshape(n_z, n_x, n_yh * ff_rows, 2, ff).transpose(0, 1, 3, 2, 4)
        block = (n_z, n_x, n_yh * run, ff)
        both = jnp.stack([up.reshape(block), down.reshape(block)])
        if l in X_FIRST:
            part, z_done = ring_scatter(both, "z", 1, 0, z_done)
        else:
            part, x_done = ring_scatter(both, "x", 2, 0, x_done)
        small[l] = part.astype(bf16)

    gains = group_exchange(jnp.stack(gain_rows).reshape(SECTIONS, 8, quarter // 8), me)
    loss_tile = jnp.full((1, 8, quarter // 8), loss_sum)
    sums = jnp.concatenate([gains, loss_tile], 0)
    for axis in ("yh", "x", "z"):
        mask = 1
        while mask < lax.axis_size(axis):
            sums = sums + swap(sums, axis, mask)
            mask *= 2
    loss_total = sums[SECTIONS, 0, 0]
    gain_total = sums[:SECTIONS].reshape(SECTIONS, width // (run * SECTIONS), run)
    gain_total = gain_total.transpose(1, 0, 2).reshape(width) / norm_gain[0]

    small_z, _ = ring_scatter(jnp.stack([small[l] for l in late]), "z", 2, 1, x_done)
    small_x, _ = ring_scatter(jnp.stack([small[l] for l in X_FIRST]), "x", 2, 1, z_done)
    summed = [
        small_x[X_FIRST.index(l)] if l in X_FIRST else small_z[late.index(l)]
        for l in range(SECTIONS)
    ]
    summed = jnp.stack(summed)
    ups = summed[:, 0].reshape(SECTIONS, n_yh, run, ff)
    downs = summed[:, 1].reshape(SECTIONS, 2, n_yh, ff_rows, ff).transpose(0, 2, 1, 3, 4)
    both = jnp.concatenate([ups, downs.reshape(SECTIONS, n_yh, run, ff)], 2)
    low, high = both[:, 0], both[:, 1]
    keep, send = jnp.where(is_low, low, high), jnp.where(is_low, high, low).astype(bf16)
    send = tied(send, (sums,))
    both = (keep + swap(send, "yh", 1).astype(f32)).astype(bf16)
    both = group_exchange(both, me)
    grad_up = both[:, :run].reshape(SECTIONS * run, ff).astype(f32) * gain_col
    down = both[:, run:].reshape(SECTIONS, 2, ff_rows, n_z // 2, span).transpose(2, 1, 3, 0, 4)
    down = down.reshape(ff_rows * n_z, SECTIONS * span)
    grad_down = matmul(down, deal, ((1,), (1,))).reshape(ff_rows, width)
    return (grad_up[None], grad_down[None], gain_total[None], loss_total)


def solution(mesh):
    sizes = (2, 2, mesh.shape["dp"] // 8, 4, 2)
    fine = Mesh(mesh.devices.reshape(sizes), ("yl", "core", "z", "x", "yh"))
    section, dp = ("yl", "core"), ("z", "x", "yh")
    return jax.shard_map(
        on_device,
        mesh=fine,
        in_specs=(
            P(dp, None),
            P(dp),
            P(dp, None),
            P(dp),
            P(),
            P(section, None),
            P(section, dp, None),
            P(section, dp, None),
        ),
        out_specs=(P(section, dp, None), P(section, dp, None), P(section, None), P()),
        check_vma=False,
    )
```

```python
import math

import jax
import jax.numpy as jnp
from jax import lax
from jax.sharding import Mesh, PartitionSpec as P

ROWS_DEV = 128
SECTIONS = 4
GATHER_GROUPS = ((1,), (2, 3))
SCATTER_GROUPS = ((2, 3), (1,))

epsilon = 1e-06
logit_cap = 15.0
f32 = jnp.float32
bf16 = jnp.bfloat16
GROUP = ("yl", "core")


def matmul(left, right, dims):
    return lax.dot_general(left, right, (dims, ((), ())), preferred_element_type=f32)


def shift(value, axis, by):
    n = lax.axis_size(axis)
    return lax.ppermute(value, axis, [(i, (i + by) % n) for i in range(n)])


def swap(value, axis, mask):
    n = lax.axis_size(axis)
    return lax.ppermute(value, axis, [(i, i ^ mask) for i in range(n)])


def halves(value, dim):
    mid = value.shape[dim] // 2
    return (
        lax.slice_in_dim(value, 0, mid, axis=dim),
        lax.slice_in_dim(value, mid, value.shape[dim], axis=dim),
    )


def tied(value, after):
    return lax.optimization_barrier((value, tuple(after)))[0] if after else value


def ring_gather(block, axis, dim, split, after=()):
    block = tied(block, after)
    n, me = lax.axis_size(axis), lax.axis_index(axis)
    shape = block.shape[:dim] + (n,) + block.shape[dim:]
    whole = jnp.zeros(shape, block.dtype)
    at_split = split + 1 if split >= dim else split

    def placed(buffer, value, member, offset=0):
        start = [0] * len(shape)
        start[dim] = member % n
        start[at_split] = offset
        return lax.dynamic_update_slice(buffer, jnp.expand_dims(value, dim), start)

    whole = placed(whole, block, me)
    up = down = block
    for step in range(1, n // 2):
        up, down = shift(up, axis, 1), shift(down, axis, -1)
        whole = placed(whole, up, me - step + n)
        whole = placed(whole, down, me + step)
    up = shift(halves(up, split)[0], axis, 1)
    down = shift(halves(down, split)[1], axis, -1)
    whole = placed(whole, up, me + n // 2)
    return placed(whole, down, me + n // 2, block.shape[split] // 2), (up, down)


def ring_scatter(parts, axis, dim, split, after=(), riders=None):
    n, me = lax.axis_size(axis), lax.axis_index(axis)

    def part(offset):
        return lax.dynamic_index_in_dim(parts, (me + offset + n) % n, dim, keepdims=False)

    def beside(up, down):
        if riders and len(riders) > 1:
            up, down, riders[0] = lax.optimization_barrier((up, down, riders.pop(1)(riders[0])))
        return up, down

    up, down = halves(tied(part(n // 2), after), split)
    up, down = beside(shift(up, axis, 1), shift(down, axis, -1))
    for step in range(n // 2 - 1, 0, -1):
        first, second = part(step).astype(f32), part(-step).astype(f32)
        if step == n // 2 - 1:
            low, high = halves(first, split)
            first = jnp.concatenate([low + up.astype(f32), high], split)
            low, high = halves(second, split)
            second = jnp.concatenate([low, high + down.astype(f32)], split)
        else:
            first, second = first + up.astype(f32), second + down.astype(f32)
        up, down = shift(first.astype(bf16), axis, 1), shift(second.astype(bf16), axis, -1)
        up, down = beside(up, down)
    return part(0).astype(f32) + up.astype(f32) + down.astype(f32), (up, down)


def group_sum(value):
    kind = value.dtype
    first = value.astype(f32) + swap(value, GROUP, 1).astype(f32)
    first = first.astype(kind)
    return first.astype(f32) + swap(first, GROUP, 2).astype(f32)


def group_exchange(blocks, me):
    def block(member):
        return lax.dynamic_index_in_dim(blocks, member, 0, keepdims=False)

    got = [block(me)] + [swap(block(me ^ mask), GROUP, mask) for mask in range(1, SECTIONS)]
    got = jnp.stack(got)
    return jnp.stack(
        [lax.dynamic_index_in_dim(got, me ^ t, 0, keepdims=False) for t in range(SECTIONS)]
    )


def head_tail(chosen, targets, scale):
    bent = jnp.tanh(chosen / logit_cap)
    logits = logit_cap * bent
    expo = jnp.exp(logits)
    summed = jnp.sum(expo, -1, keepdims=True)
    target_hot = (targets[:, None] == jnp.arange(chosen.shape[1])[None, :]).astype(f32)
    cross = jnp.log(summed[:, 0]) - jnp.sum(logits * target_hot, -1)
    loss_sum = jnp.sum(cross) / ROWS_DEV
    d_logits = (expo / summed - target_hot) / ROWS_DEV
    d_chosen = d_logits * (1.0 - bent * bent) / scale
    return (loss_sum, d_chosen)


def on_device(replay, state_ids, sampled, targets, action_table, norm_gain, w_up, w_down):
    me = lax.axis_index(GROUP)
    pos_z, pos_x, pos_yh = (lax.axis_index(a) for a in ("z", "x", "yh"))
    n_z, n_x, n_yh = (lax.axis_size(a) for a in ("z", "x", "yh"))
    dp = (pos_z * n_x + pos_x) * n_yh + pos_yh
    rows, width = replay.shape
    vocab = action_table.shape[0]
    ff = w_up.shape[2]
    quarter = width // SECTIONS
    span = quarter // n_z
    run = span // (n_x * n_yh)
    ff_rows = w_down.shape[1]

    col_in = lax.broadcasted_iota(jnp.int32, (SECTIONS * span, SECTIONS * span), 0)
    col_out = lax.broadcasted_iota(jnp.int32, (SECTIONS * span, SECTIONS * span), 1)
    t, o = col_out // span, col_out % span
    deal = (col_in == (o // run) * (run * SECTIONS) + t * run + o % run).astype(bf16)
    row_mine = lax.broadcasted_iota(jnp.int32, (SECTIONS * span, span), 0)
    o = lax.broadcasted_iota(jnp.int32, (SECTIONS * span, span), 1)
    mine = (row_mine == (o // run) * (run * SECTIONS) + me * run + o % run).astype(bf16)

    gain_col = lax.dynamic_slice_in_dim(norm_gain[0], dp * run * SECTIONS, run * SECTIONS)[:, None]
    scaled_up = (w_up[0].astype(f32) * gain_col).astype(bf16)
    up_cut = scaled_up.reshape(SECTIONS, run, ff)
    down_cut = w_down[0].reshape(ff_rows * n_z, SECTIONS * span)
    down_cut = matmul(down_cut, deal, ((1,), (0,))).astype(bf16)
    down_cut = down_cut.reshape(ff_rows, 2, n_z // 2, SECTIONS, span).transpose(3, 1, 0, 2, 4)
    down_cut = down_cut.reshape(SECTIONS, run, ff)
    layers = group_exchange(jnp.concatenate([up_cut, down_cut], 1), me)

    other = swap(layers, "yh", 1)
    is_low = pos_yh == 0
    pair = jnp.stack([jnp.where(is_low, layers, other), jnp.where(is_low, other, layers)], 1)
    ups = pair[:, :, :run].reshape(SECTIONS, n_yh * run, ff)
    downs = pair[:, :, run:].reshape(SECTIONS, n_yh, 2, ff_rows, ff).transpose(0, 2, 1, 3, 4)
    packed = jnp.stack([ups, downs.reshape(SECTIONS, n_yh * run, ff)], 1)
    small_x, x_done = ring_gather(packed[0], "x", 1, 0)
    small_z, z_done = ring_gather(packed[1:], "z", 2, 1)
    full = {}
    full[0], _ = ring_gather(small_x, "z", 1, 0)
    for group in GATHER_GROUPS:
        lo, hi = group[0], group[-1] + 1
        whole, x_done = ring_gather(small_z[lo - 1 : hi - 1], "x", 3, 1, x_done)
        for l in group:
            full[l] = whole[l - lo]
    up_full, down_full = {}, {}
    for l in range(SECTIONS):
        up_full[l] = full[l][0].reshape(quarter, ff)
        sides = full[l][1].reshape(n_z, n_x, 2, n_yh * ff_rows, ff)
        down_full[l] = jnp.concatenate(
            [sides[:, :, 0].reshape(ff, ff), sides[:, :, 1].reshape(ff, ff)], 1
        )

    both = tied(jnp.concatenate([replay, action_table], 0), (other,))
    picked = [
        matmul(both[:, i : i + SECTIONS * span], mine, ((1,), (0,))).astype(bf16)
        for i in range(0, width, SECTIONS * span)
    ]
    both = jnp.concatenate(picked, 1)
    table = both[rows:]
    local_ids = state_ids - dp * rows
    choices = jnp.arange(rows + vocab)[None, :]
    hot = (local_ids[:, None] == choices) | (sampled[:, 0:1] + rows == choices)
    state = matmul(hot.astype(bf16), both, ((1,), (0,))).astype(bf16)

    kept = []
    for l in range(SECTIONS):
        wide = state.astype(f32)
        square = jnp.sum(wide * wide, -1, keepdims=True)
        coarse = square.astype(bf16)
        fine = (square - coarse.astype(f32)).astype(bf16)
        lane = lax.broadcasted_iota(jnp.int32, (rows, 128), 1)
        extra = jnp.where(lane == 0, coarse, jnp.where(lane == 1, fine, jnp.zeros_like(fine)))
        part = matmul(state, up_full[l], ((1,), (0,)))
        total = group_sum(jnp.concatenate([part.astype(bf16), extra], 1))
        raw = total[:, :ff]
        square = total[:, ff : ff + 1] + total[:, ff + 1 : ff + 2]
        recip = lax.rsqrt(square / width + epsilon)
        upper = raw * recip
        sigm = jax.nn.sigmoid(upper)
        active = (upper * sigm).astype(bf16)
        kept.append((state, recip, raw, upper, sigm, active))
        state = (wide + matmul(active, down_full[l], ((1,), (0,)))).astype(bf16)

    scale = math.sqrt(width)
    scores = group_sum(matmul(state, table, ((1,), (1,)))) / scale
    action_hot = (sampled[:, :, None] == jnp.arange(vocab)[None, None, :]).astype(f32)
    chosen = jnp.einsum("ra,rka->rk", scores, action_hot, precision=lax.Precision.HIGHEST)
    loss_sum, d_chosen = head_tail(chosen, targets, scale)
    d_scores = jnp.einsum(
        "rk,rka->ra", d_chosen, action_hot, precision=lax.Precision.HIGHEST
    ).astype(bf16)
    grad = matmul(d_scores, table, ((1,), (0,))).astype(bf16)

    gain_rows = [None] * SECTIONS
    parts, small, large = {}, {}, {}
    x_done = ()
    for l in reversed(range(SECTIONS)):
        state, recip, raw, upper, sigm, active = kept[l]
        wide = state.astype(f32)
        d_active = group_sum(matmul(grad, down_full[l], ((1,), (1,))).astype(bf16))
        sides = [matmul(active, side, ((0,), (0,))).astype(bf16) for side in halves(grad, 1)]
        d_raw = (d_active * sigm * (1.0 + upper * (1.0 - sigm)) * recip).astype(bf16)
        up = matmul(state, d_raw, ((0,), (0,))).astype(bf16)
        mean = jnp.sum(d_raw.astype(f32) * raw, -1, keepdims=True) / width
        through = matmul(d_raw, up_full[l], ((1,), (1,)))
        gain_rows[l] = jnp.sum(through * wide, 0)
        grad = (grad.astype(f32) + through - wide * (recip * recip * mean)).astype(bf16)
        half = (n_z, n_x, n_yh * ff_rows, ff)
        down = jnp.concatenate([side.reshape(half) for side in sides], 2)
        parts[l] = jnp.stack([up.reshape(n_z, n_x, n_yh * run, ff), down])
        for group in SCATTER_GROUPS:
            if l == group[0]:
                both = jnp.stack([parts[i] for i in group])
                large[l], x_done = ring_scatter(both, "x", 3, 1, x_done)
                for i, k in enumerate(group):
                    small[k] = large[l][i].astype(bf16)

    loss_tile = jnp.full((1, 8, quarter // 8), loss_sum)
    sums = jnp.concatenate([jnp.stack(gain_rows).reshape(SECTIONS, 8, quarter // 8), loss_tile], 0)
    riders = [sums]
    for axis in ("yh", "x", "z"):
        mask = 1
        while mask < lax.axis_size(axis):
            riders.append(lambda v, axis=axis, mask=mask: v + swap(v, axis, mask))
            mask *= 2
    part, z_done = ring_scatter(parts[0], "z", 1, 0, (), riders)
    small_z = jnp.stack([small[l] for l in range(1, SECTIONS)])
    small_z, _ = ring_scatter(small_z, "z", 2, 1, x_done, riders)
    small_x, _ = ring_scatter(part.astype(bf16), "x", 1, 0)
    sums = riders[0]
    for step in riders[1:]:
        sums = step(sums)
    loss_total = sums[SECTIONS, 0, 0]
    gains = group_exchange(sums[:SECTIONS], me)
    gain_total = gains.reshape(SECTIONS, width // (run * SECTIONS), run)
    gain_total = gain_total.transpose(1, 0, 2).reshape(width) / norm_gain[0]

    summed = jnp.concatenate([small_x[None], small_z], 0)
    ups = summed[:, 0].reshape(SECTIONS, n_yh, run, ff)
    downs = summed[:, 1].reshape(SECTIONS, 2, n_yh, ff_rows, ff).transpose(0, 2, 1, 3, 4)
    both = jnp.concatenate([ups, downs.reshape(SECTIONS, n_yh, run, ff)], 2)
    low, high = both[:, 0], both[:, 1]
    keep, send = jnp.where(is_low, low, high), jnp.where(is_low, high, low).astype(bf16)
    both = (keep + swap(send, "yh", 1).astype(f32)).astype(bf16)
    both = group_exchange(both, me)
    grad_up = both[:, :run].reshape(SECTIONS * run, ff).astype(f32) * gain_col
    down = both[:, run:].reshape(SECTIONS, 2, ff_rows, n_z // 2, span).transpose(2, 1, 3, 0, 4)
    down = down.reshape(ff_rows * n_z, SECTIONS * span)
    grad_down = matmul(down, deal, ((1,), (1,))).reshape(ff_rows, width)
    return (grad_up[None], grad_down[None], gain_total[None], loss_total)


def solution(mesh):
    sizes = (2, 2, mesh.shape["dp"] // 8, 4, 2)
    fine = Mesh(mesh.devices.reshape(sizes), ("yl", "core", "z", "x", "yh"))
    section, dp = ("yl", "core"), ("z", "x", "yh")
    return jax.shard_map(
        on_device,
        mesh=fine,
        in_specs=(
            P(dp, None),
            P(dp),
            P(dp, None),
            P(dp),
            P(),
            P(section, None),
            P(section, dp, None),
            P(section, dp, None),
        ),
        out_specs=(P(section, dp, None), P(section, dp, None), P(section, None), P()),
        check_vma=False,
    )
```

```python
import math

import jax
import jax.numpy as jnp
from jax import lax
from jax.sharding import Mesh, PartitionSpec as P

ROWS_DEV = 128
SECTIONS = 4
X_FIRST = (0, 3)

epsilon = 1e-06
logit_cap = 15.0
f32 = jnp.float32
bf16 = jnp.bfloat16
GROUP = ("yl", "core")


def matmul(left, right, dims):
    return lax.dot_general(left, right, (dims, ((), ())), preferred_element_type=f32)


def shift(value, axis, by):
    n = lax.axis_size(axis)
    return lax.ppermute(value, axis, [(i, (i + by) % n) for i in range(n)])


def swap(value, axis, mask):
    n = lax.axis_size(axis)
    return lax.ppermute(value, axis, [(i, i ^ mask) for i in range(n)])


def halves(value, dim):
    mid = value.shape[dim] // 2
    return (
        lax.slice_in_dim(value, 0, mid, axis=dim),
        lax.slice_in_dim(value, mid, value.shape[dim], axis=dim),
    )


def tied(value, after):
    return lax.optimization_barrier((value, tuple(after)))[0] if after else value


def ring_gather(block, axis, dim, split, after=()):
    block = tied(block, after)
    n, me = lax.axis_size(axis), lax.axis_index(axis)
    shape = block.shape[:dim] + (n,) + block.shape[dim:]
    whole = jnp.zeros(shape, block.dtype)
    at_split = split + 1 if split >= dim else split

    def placed(buffer, value, member, offset=0):
        start = [0] * len(shape)
        start[dim] = member % n
        start[at_split] = offset
        return lax.dynamic_update_slice(buffer, jnp.expand_dims(value, dim), start)

    whole = placed(whole, block, me)
    up = down = block
    for step in range(1, n // 2):
        up, down = shift(up, axis, 1), shift(down, axis, -1)
        whole = placed(whole, up, me - step + n)
        whole = placed(whole, down, me + step)
    up = shift(halves(up, split)[0], axis, 1)
    down = shift(halves(down, split)[1], axis, -1)
    whole = placed(whole, up, me + n // 2)
    return placed(whole, down, me + n // 2, block.shape[split] // 2), (up, down)


def ring_scatter(parts, axis, dim, split, after=(), riders=None):
    n, me = lax.axis_size(axis), lax.axis_index(axis)

    def part(offset):
        return lax.dynamic_index_in_dim(parts, (me + offset + n) % n, dim, keepdims=False)

    def beside(up, down):
        step = riders.pop(1) if riders and len(riders) > 1 else None
        if step:
            up, down, riders[0] = lax.optimization_barrier((up, down, step(riders[0])))
        return up, down

    up, down = halves(tied(part(n // 2), after), split)
    up, down = beside(shift(up, axis, 1), shift(down, axis, -1))
    for step in range(n // 2 - 1, 0, -1):
        first, second = part(step).astype(f32), part(-step).astype(f32)
        if step == n // 2 - 1:
            low, high = halves(first, split)
            first = jnp.concatenate([low + up.astype(f32), high], split)
            low, high = halves(second, split)
            second = jnp.concatenate([low, high + down.astype(f32)], split)
        else:
            first, second = first + up.astype(f32), second + down.astype(f32)
        up, down = shift(first.astype(bf16), axis, 1), shift(second.astype(bf16), axis, -1)
        up, down = beside(up, down)
    return part(0).astype(f32) + up.astype(f32) + down.astype(f32), (up, down)


def added(axis):
    masks = [1 << i for i in range((lax.axis_size(axis) - 1).bit_length())]
    return [lambda v, mask=mask: v + swap(v, axis, mask) for mask in masks]


def group_sum(value):
    kind = value.dtype
    first = value.astype(f32) + swap(value, GROUP, 1).astype(f32)
    first = first.astype(kind)
    return first.astype(f32) + swap(first, GROUP, 2).astype(f32)


def group_exchange(blocks, me):
    def block(member):
        return lax.dynamic_index_in_dim(blocks, member, 0, keepdims=False)

    got = [block(me)] + [swap(block(me ^ mask), GROUP, mask) for mask in range(1, SECTIONS)]
    got = jnp.stack(got)
    return jnp.stack(
        [lax.dynamic_index_in_dim(got, me ^ t, 0, keepdims=False) for t in range(SECTIONS)]
    )


def head_tail(chosen, targets, scale):
    bent = jnp.tanh(chosen / logit_cap)
    logits = logit_cap * bent
    expo = jnp.exp(logits)
    summed = jnp.sum(expo, -1, keepdims=True)
    target_hot = (targets[:, None] == jnp.arange(chosen.shape[1])[None, :]).astype(f32)
    cross = jnp.log(summed[:, 0]) - jnp.sum(logits * target_hot, -1)
    loss_sum = jnp.sum(cross) / ROWS_DEV
    d_logits = (expo / summed - target_hot) / ROWS_DEV
    d_chosen = d_logits * (1.0 - bent * bent) / scale
    return (loss_sum, d_chosen)


def on_device(replay, state_ids, sampled, targets, action_table, norm_gain, w_up, w_down):
    me = lax.axis_index(GROUP)
    pos_z, pos_x, pos_yh = (lax.axis_index(a) for a in ("z", "x", "yh"))
    n_z, n_x, n_yh = (lax.axis_size(a) for a in ("z", "x", "yh"))
    dp = (pos_z * n_x + pos_x) * n_yh + pos_yh
    rows, width = replay.shape
    vocab = action_table.shape[0]
    ff = w_up.shape[2]
    quarter = width // SECTIONS
    span = quarter // n_z
    run = span // (n_x * n_yh)
    ff_rows = w_down.shape[1]

    col_in = lax.broadcasted_iota(jnp.int32, (SECTIONS * span, SECTIONS * span), 0)
    col_out = lax.broadcasted_iota(jnp.int32, (SECTIONS * span, SECTIONS * span), 1)
    t, o = col_out // span, col_out % span
    deal = (col_in == (o // run) * (run * SECTIONS) + t * run + o % run).astype(bf16)
    row_mine = lax.broadcasted_iota(jnp.int32, (SECTIONS * span, span), 0)
    o = lax.broadcasted_iota(jnp.int32, (SECTIONS * span, span), 1)
    mine = (row_mine == (o // run) * (run * SECTIONS) + me * run + o % run).astype(bf16)

    gain_col = lax.dynamic_slice_in_dim(norm_gain[0], dp * run * SECTIONS, run * SECTIONS)[:, None]
    scaled_up = (w_up[0].astype(f32) * gain_col).astype(bf16)
    up_cut = scaled_up.reshape(SECTIONS, run, ff)
    down_cut = w_down[0].reshape(ff_rows * n_z, SECTIONS * span)
    down_cut = matmul(down_cut, deal, ((1,), (0,))).astype(bf16)
    down_cut = down_cut.reshape(ff_rows, 2, n_z // 2, SECTIONS, span).transpose(3, 1, 0, 2, 4)
    down_cut = down_cut.reshape(SECTIONS, run, ff)
    layers = group_exchange(jnp.concatenate([up_cut, down_cut], 1), me)

    other = swap(layers, "yh", 1)
    is_low = pos_yh == 0
    pair = jnp.stack([jnp.where(is_low, layers, other), jnp.where(is_low, other, layers)], 1)
    ups = pair[:, :, :run].reshape(SECTIONS, n_yh * run, ff)
    downs = pair[:, :, run:].reshape(SECTIONS, n_yh, 2, ff_rows, ff).transpose(0, 2, 1, 3, 4)
    packed = jnp.stack([ups, downs.reshape(SECTIONS, n_yh * run, ff)], 1)
    late = [l for l in range(SECTIONS) if l not in X_FIRST]
    small_x, _ = ring_gather(jnp.stack([packed[l] for l in X_FIRST]), "x", 2, 1)
    small_z, _ = ring_gather(jnp.stack([packed[l] for l in late]), "z", 2, 1)
    full = {}
    x_done = z_done = ()
    for l in range(SECTIONS):
        if l in X_FIRST:
            full[l], z_done = ring_gather(small_x[X_FIRST.index(l)], "z", 1, 0, z_done)
        else:
            full[l], x_done = ring_gather(small_z[late.index(l)], "x", 2, 0, x_done)
    up_full, down_full = {}, {}
    for l in range(SECTIONS):
        up_full[l] = full[l][0].reshape(quarter, ff)
        sides = full[l][1].reshape(n_z, n_x, 2, n_yh * ff_rows, ff)
        down_full[l] = jnp.concatenate(
            [sides[:, :, 0].reshape(ff, ff), sides[:, :, 1].reshape(ff, ff)], 1
        )

    both = tied(jnp.concatenate([replay, action_table], 0), (other,))
    picked = [
        matmul(both[:, i : i + SECTIONS * span], mine, ((1,), (0,))).astype(bf16)
        for i in range(0, width, SECTIONS * span)
    ]
    both = jnp.concatenate(picked, 1)
    table = both[rows:]
    local_ids = state_ids - dp * rows
    choices = jnp.arange(rows + vocab)[None, :]
    hot = (local_ids[:, None] == choices) | (sampled[:, 0:1] + rows == choices)
    state = matmul(hot.astype(bf16), both, ((1,), (0,))).astype(bf16)

    kept = []
    for l in range(SECTIONS):
        wide = state.astype(f32)
        square = jnp.sum(wide * wide, -1, keepdims=True)
        coarse = square.astype(bf16)
        fine = (square - coarse.astype(f32)).astype(bf16)
        lane = lax.broadcasted_iota(jnp.int32, (rows, 128), 1)
        extra = jnp.where(lane == 0, coarse, jnp.where(lane == 1, fine, jnp.zeros_like(fine)))
        part = matmul(state, up_full[l], ((1,), (0,)))
        total = group_sum(jnp.concatenate([part.astype(bf16), extra], 1))
        raw = total[:, :ff]
        square = total[:, ff : ff + 1] + total[:, ff + 1 : ff + 2]
        recip = lax.rsqrt(square / width + epsilon)
        upper = raw * recip
        sigm = jax.nn.sigmoid(upper)
        active = (upper * sigm).astype(bf16)
        kept.append((state, recip, raw, upper, sigm, active))
        state = (wide + matmul(active, down_full[l], ((1,), (0,)))).astype(bf16)

    scale = math.sqrt(width)
    scores = group_sum(matmul(state, table, ((1,), (1,)))) / scale
    action_hot = (sampled[:, :, None] == jnp.arange(vocab)[None, None, :]).astype(f32)
    chosen = jnp.einsum("ra,rka->rk", scores, action_hot, precision=lax.Precision.HIGHEST)
    loss_sum, d_chosen = head_tail(chosen, targets, scale)
    d_scores = jnp.einsum(
        "rk,rka->ra", d_chosen, action_hot, precision=lax.Precision.HIGHEST
    ).astype(bf16)
    grad = matmul(d_scores, table, ((1,), (0,))).astype(bf16)

    gain_rows = [None] * SECTIONS
    small = {}
    x_done = z_done = ()
    for l in reversed(range(SECTIONS)):
        state, recip, raw, upper, sigm, active = kept[l]
        wide = state.astype(f32)
        d_active = group_sum(matmul(grad, down_full[l], ((1,), (1,))).astype(bf16))
        sides = [matmul(active, side, ((0,), (0,))).astype(bf16) for side in halves(grad, 1)]
        d_raw = (d_active * sigm * (1.0 + upper * (1.0 - sigm)) * recip).astype(bf16)
        up = matmul(state, d_raw, ((0,), (0,))).astype(bf16)
        mean = jnp.sum(d_raw.astype(f32) * raw, -1, keepdims=True) / width
        through = matmul(d_raw, up_full[l], ((1,), (1,)))
        gain_rows[l] = jnp.sum(through * wide, 0)
        grad = (grad.astype(f32) + through - wide * (recip * recip * mean)).astype(bf16)
        half = (n_z, n_x, n_yh * ff_rows, ff)
        down = jnp.concatenate([side.reshape(half) for side in sides], 2)
        both = jnp.stack([up.reshape(n_z, n_x, n_yh * run, ff), down])
        riders = None
        if l == 0:
            loss_tile = jnp.full((1, 8, quarter // 8), loss_sum)
            gains = jnp.stack(gain_rows).reshape(SECTIONS, 8, quarter // 8)
            riders = [jnp.concatenate([gains, loss_tile], 0)] + added("x")
        if l in X_FIRST:
            part, z_done = ring_scatter(both, "z", 1, 0, z_done, riders)
        else:
            part, x_done = ring_scatter(both, "x", 2, 0, x_done, riders)
        small[l] = part.astype(bf16)

    riders = [riders[0], None] + added("z")
    small_z, _ = ring_scatter(jnp.stack([small[l] for l in late]), "z", 2, 1, (), riders)
    small_x, _ = ring_scatter(jnp.stack([small[l] for l in X_FIRST]), "x", 2, 1)
    summed = [
        small_x[X_FIRST.index(l)] if l in X_FIRST else small_z[late.index(l)]
        for l in range(SECTIONS)
    ]
    summed = jnp.stack(summed)
    ups = summed[:, 0].reshape(SECTIONS, n_yh, run, ff)
    downs = summed[:, 1].reshape(SECTIONS, 2, n_yh, ff_rows, ff).transpose(0, 2, 1, 3, 4)
    both = jnp.concatenate([ups, downs.reshape(SECTIONS, n_yh, run, ff)], 2)
    low, high = both[:, 0], both[:, 1]
    keep, send = jnp.where(is_low, low, high), jnp.where(is_low, high, low).astype(bf16)
    send, sums = lax.optimization_barrier((send, riders[0]))
    both = (keep + swap(send, "yh", 1).astype(f32)).astype(bf16)
    sums = sums + swap(sums, "yh", 1)
    loss_total = sums[SECTIONS, 0, 0]
    both, sums = lax.optimization_barrier((both, sums))
    both = group_exchange(both, me)
    gains = group_exchange(sums[:SECTIONS], me)
    gain_total = gains.reshape(SECTIONS, width // (run * SECTIONS), run)
    gain_total = gain_total.transpose(1, 0, 2).reshape(width) / norm_gain[0]
    grad_up = both[:, :run].reshape(SECTIONS * run, ff).astype(f32) * gain_col
    down = both[:, run:].reshape(SECTIONS, 2, ff_rows, n_z // 2, span).transpose(2, 1, 3, 0, 4)
    down = down.reshape(ff_rows * n_z, SECTIONS * span)
    grad_down = matmul(down, deal, ((1,), (1,))).reshape(ff_rows, width)
    return (grad_up[None], grad_down[None], gain_total[None], loss_total)


def solution(mesh):
    sizes = (2, 2, mesh.shape["dp"] // 8, 4, 2)
    fine = Mesh(mesh.devices.reshape(sizes), ("yl", "core", "z", "x", "yh"))
    section, dp = ("yl", "core"), ("z", "x", "yh")
    return jax.shard_map(
        on_device,
        mesh=fine,
        in_specs=(
            P(dp, None),
            P(dp),
            P(dp, None),
            P(dp),
            P(),
            P(section, None),
            P(section, dp, None),
            P(section, dp, None),
        ),
        out_specs=(P(section, dp, None), P(section, dp, None), P(section, None), P()),
        check_vma=False,
    )
```

```python
import math

import jax
import jax.numpy as jnp
from jax import lax
from jax.sharding import Mesh, PartitionSpec as P

ROWS_DEV = 128
SECTIONS = 4
X_FIRST = (0, 3)

epsilon = 1e-06
logit_cap = 15.0
f32 = jnp.float32
bf16 = jnp.bfloat16
GROUP = ("yl", "core")


def matmul(left, right, dims):
    return lax.dot_general(left, right, (dims, ((), ())), preferred_element_type=f32)


def shift(value, axis, by):
    n = lax.axis_size(axis)
    return lax.ppermute(value, axis, [(i, (i + by) % n) for i in range(n)])


def swap(value, axis, mask):
    n = lax.axis_size(axis)
    return lax.ppermute(value, axis, [(i, i ^ mask) for i in range(n)])


def halves(value, dim):
    mid = value.shape[dim] // 2
    return (
        lax.slice_in_dim(value, 0, mid, axis=dim),
        lax.slice_in_dim(value, mid, value.shape[dim], axis=dim),
    )


def tied(value, after):
    return lax.optimization_barrier((value, tuple(after)))[0] if after else value


def ring_gather(block, axis, dim, split, after=()):
    block = tied(block, after)
    n, me = lax.axis_size(axis), lax.axis_index(axis)
    shape = block.shape[:dim] + (n,) + block.shape[dim:]
    whole = jnp.zeros(shape, block.dtype)
    at_split = split + 1 if split >= dim else split

    def placed(buffer, value, member, offset=0):
        start = [0] * len(shape)
        start[dim] = member % n
        start[at_split] = offset
        return lax.dynamic_update_slice(buffer, jnp.expand_dims(value, dim), start)

    whole = placed(whole, block, me)
    up = down = block
    arrivals = []
    for step in range(1, n // 2):
        up, down = lax.optimization_barrier((shift(up, axis, 1), shift(down, axis, -1)))
        arrivals.append((up, down))
        whole = placed(whole, up, me - step + n)
        whole = placed(whole, down, me + step)
    up = shift(halves(up, split)[0], axis, 1)
    down = shift(halves(down, split)[1], axis, -1)
    arrivals.append((up, down))
    whole = placed(whole, up, me + n // 2)
    return placed(whole, down, me + n // 2, block.shape[split] // 2), arrivals


def ring_scatter(parts, axis, dim, split, after=(), riders=None):
    n, me = lax.axis_size(axis), lax.axis_index(axis)

    def part(offset):
        return lax.dynamic_index_in_dim(parts, (me + offset + n) % n, dim, keepdims=False)

    def beside(up, down):
        if riders and len(riders) > 1:
            up, down, value = lax.optimization_barrier((up, down, riders[0]))
            riders[0] = riders.pop(1)(value)
            return up, down
        return lax.optimization_barrier((up, down))

    up, down = halves(tied(part(n // 2), after), split)
    up, down = beside(shift(up, axis, 1), shift(down, axis, -1))
    for step in range(n // 2 - 1, 0, -1):
        first, second = part(step).astype(f32), part(-step).astype(f32)
        if step == n // 2 - 1:
            low, high = halves(first, split)
            first = jnp.concatenate([low + up.astype(f32), high], split)
            low, high = halves(second, split)
            second = jnp.concatenate([low, high + down.astype(f32)], split)
        else:
            first, second = first + up.astype(f32), second + down.astype(f32)
        up, down = shift(first.astype(bf16), axis, 1), shift(second.astype(bf16), axis, -1)
        up, down = beside(up, down)
    return part(0).astype(f32) + up.astype(f32) + down.astype(f32), (up, down)


def added(axis):
    masks = [1 << i for i in range((lax.axis_size(axis) - 1).bit_length())]
    return [lambda v, mask=mask: v + swap(v, axis, mask) for mask in masks]


def group_sum(value):
    kind = value.dtype
    first = value.astype(f32) + swap(value, GROUP, 1).astype(f32)
    first = first.astype(kind)
    return first.astype(f32) + swap(first, GROUP, 2).astype(f32)


def group_exchange(blocks, me):
    def block(member):
        return lax.dynamic_index_in_dim(blocks, member, 0, keepdims=False)

    got = [block(me)] + [swap(block(me ^ mask), GROUP, mask) for mask in range(1, SECTIONS)]
    got = jnp.stack(got)
    return jnp.stack(
        [lax.dynamic_index_in_dim(got, me ^ t, 0, keepdims=False) for t in range(SECTIONS)]
    )


def head_tail(chosen, targets, scale):
    bent = jnp.tanh(chosen / logit_cap)
    logits = logit_cap * bent
    expo = jnp.exp(logits)
    summed = jnp.sum(expo, -1, keepdims=True)
    target_hot = (targets[:, None] == jnp.arange(chosen.shape[1])[None, :]).astype(f32)
    cross = jnp.log(summed[:, 0]) - jnp.sum(logits * target_hot, -1)
    loss_sum = jnp.sum(cross) / ROWS_DEV
    d_logits = (expo / summed - target_hot) / ROWS_DEV
    d_chosen = d_logits * (1.0 - bent * bent) / scale
    return (loss_sum, d_chosen)


def on_device(replay, state_ids, sampled, targets, action_table, norm_gain, w_up, w_down):
    me = lax.axis_index(GROUP)
    pos_z, pos_x, pos_yh = (lax.axis_index(a) for a in ("z", "x", "yh"))
    n_z, n_x, n_yh = (lax.axis_size(a) for a in ("z", "x", "yh"))
    dp = (pos_z * n_x + pos_x) * n_yh + pos_yh
    rows, width = replay.shape
    vocab = action_table.shape[0]
    ff = w_up.shape[2]
    quarter = width // SECTIONS
    span = quarter // n_z
    run = span // (n_x * n_yh)
    ff_rows = w_down.shape[1]

    col_in = lax.broadcasted_iota(jnp.int32, (SECTIONS * span, SECTIONS * span), 0)
    col_out = lax.broadcasted_iota(jnp.int32, (SECTIONS * span, SECTIONS * span), 1)
    t, o = col_out // span, col_out % span
    deal = (col_in == (o // run) * (run * SECTIONS) + t * run + o % run).astype(bf16)
    row_mine = lax.broadcasted_iota(jnp.int32, (SECTIONS * span, span), 0)
    o = lax.broadcasted_iota(jnp.int32, (SECTIONS * span, span), 1)
    mine = (row_mine == (o // run) * (run * SECTIONS) + me * run + o % run).astype(bf16)

    gain_col = lax.dynamic_slice_in_dim(norm_gain[0], dp * run * SECTIONS, run * SECTIONS)[:, None]
    scaled_up = (w_up[0].astype(f32) * gain_col).astype(bf16)
    up_cut = scaled_up.reshape(SECTIONS, run, ff)
    down_cut = w_down[0].reshape(ff_rows * n_z, SECTIONS * span)
    down_cut = matmul(down_cut, deal, ((1,), (0,))).astype(bf16)
    down_cut = down_cut.reshape(ff_rows, 2, n_z // 2, SECTIONS, span).transpose(3, 1, 0, 2, 4)
    down_cut = down_cut.reshape(SECTIONS, run, ff)
    layers = group_exchange(jnp.concatenate([up_cut, down_cut], 1), me)

    other = swap(layers, "yh", 1)
    is_low = pos_yh == 0
    pair = jnp.stack([jnp.where(is_low, layers, other), jnp.where(is_low, other, layers)], 1)
    ups = pair[:, :, :run].reshape(SECTIONS, n_yh * run, ff)
    downs = pair[:, :, run:].reshape(SECTIONS, n_yh, 2, ff_rows, ff).transpose(0, 2, 1, 3, 4)
    packed = jnp.stack([ups, downs.reshape(SECTIONS, n_yh * run, ff)], 1)
    late = [l for l in range(SECTIONS) if l not in X_FIRST]
    small_x, _ = ring_gather(jnp.stack([packed[l] for l in X_FIRST]), "x", 2, 1)
    small_z, _ = ring_gather(jnp.stack([packed[l] for l in late]), "z", 2, 1)
    full = {}
    whole, x_arrivals = ring_gather(small_z, "x", 3, 1)
    z_done = ()
    for i, l in enumerate(X_FIRST):
        full[l], z_arrivals = ring_gather(small_x[i], "z", 1, 0, z_done)
        z_done = z_arrivals[-1] + x_arrivals[0]
    for i, l in enumerate(late):
        full[l] = whole[i]
    full[0] = tied(full[0], x_arrivals[0])

    up_full, down_full = {}, {}
    for l in range(SECTIONS):
        up_full[l] = full[l][0].reshape(quarter, ff)
        sides = full[l][1].reshape(n_z, n_x, 2, n_yh * ff_rows, ff)
        down_full[l] = jnp.concatenate(
            [sides[:, :, 0].reshape(ff, ff), sides[:, :, 1].reshape(ff, ff)], 1
        )

    both = tied(jnp.concatenate([replay, action_table], 0), (other,))
    picked = [
        matmul(both[:, i : i + SECTIONS * span], mine, ((1,), (0,))).astype(bf16)
        for i in range(0, width, SECTIONS * span)
    ]
    both = jnp.concatenate(picked, 1)
    table = both[rows:]
    local_ids = state_ids - dp * rows
    choices = jnp.arange(rows + vocab)[None, :]
    hot = (local_ids[:, None] == choices) | (sampled[:, 0:1] + rows == choices)
    state = matmul(hot.astype(bf16), both, ((1,), (0,))).astype(bf16)

    kept = []
    for l in range(SECTIONS):
        wide = state.astype(f32)
        square = jnp.sum(wide * wide, -1, keepdims=True)
        coarse = square.astype(bf16)
        fine = (square - coarse.astype(f32)).astype(bf16)
        lane = lax.broadcasted_iota(jnp.int32, (rows, 128), 1)
        extra = jnp.where(lane == 0, coarse, jnp.where(lane == 1, fine, jnp.zeros_like(fine)))
        part = matmul(state, up_full[l], ((1,), (0,)))
        total = group_sum(jnp.concatenate([part.astype(bf16), extra], 1))
        raw = total[:, :ff]
        square = total[:, ff : ff + 1] + total[:, ff + 1 : ff + 2]
        recip = lax.rsqrt(square / width + epsilon)
        upper = raw * recip
        sigm = jax.nn.sigmoid(upper)
        active = (upper * sigm).astype(bf16)
        kept.append((state, recip, raw, upper, sigm, active))
        state = (wide + matmul(active, down_full[l], ((1,), (0,)))).astype(bf16)

    scale = math.sqrt(width)
    scores = group_sum(matmul(state, table, ((1,), (1,)))) / scale
    action_hot = (sampled[:, :, None] == jnp.arange(vocab)[None, None, :]).astype(f32)
    chosen = jnp.einsum("ra,rka->rk", scores, action_hot, precision=lax.Precision.HIGHEST)
    loss_sum, d_chosen = head_tail(chosen, targets, scale)
    d_scores = jnp.einsum(
        "rk,rka->ra", d_chosen, action_hot, precision=lax.Precision.HIGHEST
    ).astype(bf16)
    grad = matmul(d_scores, table, ((1,), (0,))).astype(bf16)

    gain_rows = [None] * SECTIONS
    parts, small = {}, {}
    x_done = z_done = ()
    for l in reversed(range(SECTIONS)):
        state, recip, raw, upper, sigm, active = kept[l]
        wide = state.astype(f32)
        d_active = group_sum(matmul(grad, down_full[l], ((1,), (1,))).astype(bf16))
        sides = [matmul(active, side, ((0,), (0,))).astype(bf16) for side in halves(grad, 1)]
        d_raw = (d_active * sigm * (1.0 + upper * (1.0 - sigm)) * recip).astype(bf16)
        up = matmul(state, d_raw, ((0,), (0,))).astype(bf16)
        mean = jnp.sum(d_raw.astype(f32) * raw, -1, keepdims=True) / width
        through = matmul(d_raw, up_full[l], ((1,), (1,)))
        gain_rows[l] = jnp.sum(through * wide, 0)
        grad = (grad.astype(f32) + through - wide * (recip * recip * mean)).astype(bf16)
        half = (n_z, n_x, n_yh * ff_rows, ff)
        down = jnp.concatenate([side.reshape(half) for side in sides], 2)
        parts[l] = jnp.stack([up.reshape(n_z, n_x, n_yh * run, ff), down])
        riders = None
        if l == 0:
            loss_tile = jnp.full((1, 8, quarter // 8), loss_sum)
            gains = jnp.stack(gain_rows).reshape(SECTIONS, 8, quarter // 8)
            riders = [jnp.concatenate([gains, loss_tile], 0)] + added("x") + added("z")
        if l in X_FIRST:
            part, z_done = ring_scatter(parts[l], "z", 1, 0, z_done, riders)
            small[l] = part.astype(bf16)
        else:
            part, x_done = ring_scatter(parts[l], "x", 2, 0, x_done)
            small[l] = part.astype(bf16)

    small_z = jnp.stack([small[l] for l in late])
    small_z, _ = ring_scatter(small_z, "z", 2, 1, (), riders)
    small_x, _ = ring_scatter(jnp.stack([small[l] for l in X_FIRST]), "x", 2, 1)
    summed = [
        small_x[X_FIRST.index(l)] if l in X_FIRST else small_z[late.index(l)]
        for l in range(SECTIONS)
    ]
    summed = jnp.stack(summed)
    ups = summed[:, 0].reshape(SECTIONS, n_yh, run, ff)
    downs = summed[:, 1].reshape(SECTIONS, 2, n_yh, ff_rows, ff).transpose(0, 2, 1, 3, 4)
    both = jnp.concatenate([ups, downs.reshape(SECTIONS, n_yh, run, ff)], 2)
    low, high = both[:, 0], both[:, 1]
    keep, send = jnp.where(is_low, low, high), jnp.where(is_low, high, low).astype(bf16)
    send, sums = lax.optimization_barrier((send, riders[0]))
    both = (keep + swap(send, "yh", 1).astype(f32)).astype(bf16)
    sums = sums + swap(sums, "yh", 1)
    loss_total = sums[SECTIONS, 0, 0]
    both, sums = lax.optimization_barrier((both, sums))
    both = group_exchange(both, me)
    gains = group_exchange(sums[:SECTIONS], me)
    gain_total = gains.reshape(SECTIONS, width // (run * SECTIONS), run)
    gain_total = gain_total.transpose(1, 0, 2).reshape(width) / norm_gain[0]
    grad_up = both[:, :run].reshape(SECTIONS * run, ff).astype(f32) * gain_col
    down = both[:, run:].reshape(SECTIONS, 2, ff_rows, n_z // 2, span).transpose(2, 1, 3, 0, 4)
    down = down.reshape(ff_rows * n_z, SECTIONS * span)
    grad_down = matmul(down, deal, ((1,), (1,))).reshape(ff_rows, width)
    return (grad_up[None], grad_down[None], gain_total[None], loss_total)


def solution(mesh):
    sizes = (2, 2, mesh.shape["dp"] // 8, 4, 2)
    fine = Mesh(mesh.devices.reshape(sizes), ("yl", "core", "z", "x", "yh"))
    section, dp = ("yl", "core"), ("z", "x", "yh")
    return jax.shard_map(
        on_device,
        mesh=fine,
        in_specs=(
            P(dp, None),
            P(dp),
            P(dp, None),
            P(dp),
            P(),
            P(section, None),
            P(section, dp, None),
            P(section, dp, None),
        ),
        out_specs=(P(section, dp, None), P(section, dp, None), P(section, None), P()),
        check_vma=False,
    )
```

```python
import math

import jax
import jax.numpy as jnp
from jax import lax
from jax.sharding import Mesh, PartitionSpec as P

ROWS_DEV = 128
SECTIONS = 4
X_FIRST = (0, 3)

epsilon = 1e-06
logit_cap = 15.0
f32 = jnp.float32
bf16 = jnp.bfloat16
GROUP = ("yl", "core")


def matmul(left, right, dims):
    return lax.dot_general(left, right, (dims, ((), ())), preferred_element_type=f32)


def shift(value, axis, by):
    n = lax.axis_size(axis)
    return lax.ppermute(value, axis, [(i, (i + by) % n) for i in range(n)])


def swap(value, axis, mask):
    n = lax.axis_size(axis)
    return lax.ppermute(value, axis, [(i, i ^ mask) for i in range(n)])


def halves(value, dim):
    mid = value.shape[dim] // 2
    return (
        lax.slice_in_dim(value, 0, mid, axis=dim),
        lax.slice_in_dim(value, mid, value.shape[dim], axis=dim),
    )


def tied(value, after):
    return lax.optimization_barrier((value, tuple(after)))[0] if after else value


def ring_gather(block, axis, dim, split, after=(), gate=()):
    block = tied(block, after)
    n, me = lax.axis_size(axis), lax.axis_index(axis)
    shape = block.shape[:dim] + (n,) + block.shape[dim:]
    whole = jnp.zeros(shape, block.dtype)
    at_split = split + 1 if split >= dim else split

    def placed(buffer, value, member, offset=0):
        start = [0] * len(shape)
        start[dim] = member % n
        start[at_split] = offset
        return lax.dynamic_update_slice(buffer, jnp.expand_dims(value, dim), start)

    whole = placed(whole, block, me)
    up = down = block
    arrivals = []
    for step in range(1, n // 2):
        up, down = lax.optimization_barrier((shift(up, axis, 1), shift(down, axis, -1)))
        arrivals.append((up, down))
        whole = placed(whole, up, me - step + n)
        whole = placed(whole, down, me + step)
    up, down = tied((up, down), gate)
    up = shift(halves(up, split)[0], axis, 1)
    down = shift(halves(down, split)[1], axis, -1)
    arrivals.append((up, down))
    whole = placed(whole, up, me + n // 2)
    return placed(whole, down, me + n // 2, block.shape[split] // 2), arrivals


def ring_scatter(parts, axis, dim, split, after=(), riders=None):
    n, me = lax.axis_size(axis), lax.axis_index(axis)

    def part(offset):
        return lax.dynamic_index_in_dim(parts, (me + offset + n) % n, dim, keepdims=False)

    def beside(up, down):
        if riders and len(riders) > 1:
            up, down, value = lax.optimization_barrier((up, down, riders[0]))
            riders[0] = riders.pop(1)(value)
            return up, down
        return lax.optimization_barrier((up, down))

    up, down = halves(tied(part(n // 2), after), split)
    up, down = beside(shift(up, axis, 1), shift(down, axis, -1))
    for step in range(n // 2 - 1, 0, -1):
        first, second = part(step).astype(f32), part(-step).astype(f32)
        if step == n // 2 - 1:
            low, high = halves(first, split)
            first = jnp.concatenate([low + up.astype(f32), high], split)
            low, high = halves(second, split)
            second = jnp.concatenate([low, high + down.astype(f32)], split)
        else:
            first, second = first + up.astype(f32), second + down.astype(f32)
        up, down = shift(first.astype(bf16), axis, 1), shift(second.astype(bf16), axis, -1)
        up, down = beside(up, down)
    return part(0).astype(f32) + up.astype(f32) + down.astype(f32), (up, down)


def added(axis):
    masks = [1 << i for i in range((lax.axis_size(axis) - 1).bit_length())]
    return [lambda v, mask=mask: v + swap(v, axis, mask) for mask in masks]


def group_sum(value):
    kind = value.dtype
    first = value.astype(f32) + swap(value, GROUP, 1).astype(f32)
    first = first.astype(kind)
    return first.astype(f32) + swap(first, GROUP, 2).astype(f32)


def group_exchange(blocks, me):
    def block(member):
        return lax.dynamic_index_in_dim(blocks, member, 0, keepdims=False)

    got = [block(me)] + [swap(block(me ^ mask), GROUP, mask) for mask in range(1, SECTIONS)]
    got = jnp.stack(got)
    return jnp.stack(
        [lax.dynamic_index_in_dim(got, me ^ t, 0, keepdims=False) for t in range(SECTIONS)]
    )


def head_tail(chosen, targets, scale):
    bent = jnp.tanh(chosen / logit_cap)
    logits = logit_cap * bent
    expo = jnp.exp(logits)
    summed = jnp.sum(expo, -1, keepdims=True)
    target_hot = (targets[:, None] == jnp.arange(chosen.shape[1])[None, :]).astype(f32)
    cross = jnp.log(summed[:, 0]) - jnp.sum(logits * target_hot, -1)
    loss_sum = jnp.sum(cross) / ROWS_DEV
    d_logits = (expo / summed - target_hot) / ROWS_DEV
    d_chosen = d_logits * (1.0 - bent * bent) / scale
    return (loss_sum, d_chosen)


def on_device(replay, state_ids, sampled, targets, action_table, norm_gain, w_up, w_down):
    me = lax.axis_index(GROUP)
    pos_z, pos_x, pos_yh = (lax.axis_index(a) for a in ("z", "x", "yh"))
    n_z, n_x, n_yh = (lax.axis_size(a) for a in ("z", "x", "yh"))
    dp = (pos_z * n_x + pos_x) * n_yh + pos_yh
    rows, width = replay.shape
    vocab = action_table.shape[0]
    ff = w_up.shape[2]
    quarter = width // SECTIONS
    span = quarter // n_z
    run = span // (n_x * n_yh)
    ff_rows = w_down.shape[1]

    col_in = lax.broadcasted_iota(jnp.int32, (SECTIONS * span, SECTIONS * span), 0)
    col_out = lax.broadcasted_iota(jnp.int32, (SECTIONS * span, SECTIONS * span), 1)
    t, o = col_out // span, col_out % span
    deal = (col_in == (o // run) * (run * SECTIONS) + t * run + o % run).astype(bf16)
    row_mine = lax.broadcasted_iota(jnp.int32, (SECTIONS * span, span), 0)
    o = lax.broadcasted_iota(jnp.int32, (SECTIONS * span, span), 1)
    mine = (row_mine == (o // run) * (run * SECTIONS) + me * run + o % run).astype(bf16)

    gain_col = lax.dynamic_slice_in_dim(norm_gain[0], dp * run * SECTIONS, run * SECTIONS)[:, None]
    scaled_up = (w_up[0].astype(f32) * gain_col).astype(bf16)
    up_cut = scaled_up.reshape(SECTIONS, run, ff)
    down_cut = w_down[0].reshape(ff_rows * n_z, SECTIONS * span)
    down_cut = matmul(down_cut, deal, ((1,), (0,))).astype(bf16)
    down_cut = down_cut.reshape(ff_rows, 2, n_z // 2, SECTIONS, span).transpose(3, 1, 0, 2, 4)
    down_cut = down_cut.reshape(SECTIONS, run, ff)
    layers = group_exchange(jnp.concatenate([up_cut, down_cut], 1), me)

    other = swap(layers, "yh", 1)
    is_low = pos_yh == 0
    pair = jnp.stack([jnp.where(is_low, layers, other), jnp.where(is_low, other, layers)], 1)
    ups = pair[:, :, :run].reshape(SECTIONS, n_yh * run, ff)
    downs = pair[:, :, run:].reshape(SECTIONS, n_yh, 2, ff_rows, ff).transpose(0, 2, 1, 3, 4)
    packed = jnp.stack([ups, downs.reshape(SECTIONS, n_yh * run, ff)], 1)
    late = [l for l in range(SECTIONS) if l not in X_FIRST]
    small_x, _ = ring_gather(jnp.stack([packed[l] for l in X_FIRST]), "x", 2, 1)
    full = {}
    first, last = X_FIRST
    full[first], z_arrivals = ring_gather(small_x[0], "z", 1, 0)
    small_z = jnp.stack([packed[l] for l in late])
    small_z, _ = ring_gather(small_z, "z", 2, 1, (), z_arrivals[0])
    whole, x_arrivals = ring_gather(small_z, "x", 3, 1, z_arrivals[1])
    for i, l in enumerate(late):
        full[l] = whole[i]
    full[last], _ = ring_gather(small_x[1], "z", 1, 0, z_arrivals[-1] + x_arrivals[0])
    up_full, down_full = {}, {}
    for l in range(SECTIONS):
        up_full[l] = full[l][0].reshape(quarter, ff)
        sides = full[l][1].reshape(n_z, n_x, 2, n_yh * ff_rows, ff)
        down_full[l] = jnp.concatenate(
            [sides[:, :, 0].reshape(ff, ff), sides[:, :, 1].reshape(ff, ff)], 1
        )
    down_full[0] = tied(down_full[0], x_arrivals[0])

    both = tied(jnp.concatenate([replay, action_table], 0), (other,))
    picked = [
        matmul(both[:, i : i + SECTIONS * span], mine, ((1,), (0,))).astype(bf16)
        for i in range(0, width, SECTIONS * span)
    ]
    both = jnp.concatenate(picked, 1)
    table = both[rows:]
    local_ids = state_ids - dp * rows
    choices = jnp.arange(rows + vocab)[None, :]
    hot = (local_ids[:, None] == choices) | (sampled[:, 0:1] + rows == choices)
    state = matmul(hot.astype(bf16), both, ((1,), (0,))).astype(bf16)

    kept = []
    for l in range(SECTIONS):
        wide = state.astype(f32)
        square = jnp.sum(wide * wide, -1, keepdims=True)
        coarse = square.astype(bf16)
        fine = (square - coarse.astype(f32)).astype(bf16)
        lane = lax.broadcasted_iota(jnp.int32, (rows, 128), 1)
        extra = jnp.where(lane == 0, coarse, jnp.where(lane == 1, fine, jnp.zeros_like(fine)))
        part = matmul(state, up_full[l], ((1,), (0,)))
        total = group_sum(jnp.concatenate([part.astype(bf16), extra], 1))
        raw = total[:, :ff]
        square = total[:, ff : ff + 1] + total[:, ff + 1 : ff + 2]
        recip = lax.rsqrt(square / width + epsilon)
        upper = raw * recip
        sigm = jax.nn.sigmoid(upper)
        active = (upper * sigm).astype(bf16)
        kept.append((state, recip, raw, upper, sigm, active))
        state = (wide + matmul(active, down_full[l], ((1,), (0,)))).astype(bf16)

    scale = math.sqrt(width)
    scores = group_sum(matmul(state, table, ((1,), (1,)))) / scale
    action_hot = (sampled[:, :, None] == jnp.arange(vocab)[None, None, :]).astype(f32)
    chosen = jnp.einsum("ra,rka->rk", scores, action_hot, precision=lax.Precision.HIGHEST)
    loss_sum, d_chosen = head_tail(chosen, targets, scale)
    d_scores = jnp.einsum(
        "rk,rka->ra", d_chosen, action_hot, precision=lax.Precision.HIGHEST
    ).astype(bf16)
    grad = matmul(d_scores, table, ((1,), (0,))).astype(bf16)

    gain_rows = [None] * SECTIONS
    parts, small = {}, {}
    x_done = z_done = ()
    for l in reversed(range(SECTIONS)):
        state, recip, raw, upper, sigm, active = kept[l]
        wide = state.astype(f32)
        d_active = group_sum(matmul(grad, down_full[l], ((1,), (1,))).astype(bf16))
        sides = [matmul(active, side, ((0,), (0,))).astype(bf16) for side in halves(grad, 1)]
        d_raw = (d_active * sigm * (1.0 + upper * (1.0 - sigm)) * recip).astype(bf16)
        up = matmul(state, d_raw, ((0,), (0,))).astype(bf16)
        mean = jnp.sum(d_raw.astype(f32) * raw, -1, keepdims=True) / width
        through = matmul(d_raw, up_full[l], ((1,), (1,)))
        gain_rows[l] = jnp.sum(through * wide, 0)
        grad = (grad.astype(f32) + through - wide * (recip * recip * mean)).astype(bf16)
        half = (n_z, n_x, n_yh * ff_rows, ff)
        down = jnp.concatenate([side.reshape(half) for side in sides], 2)
        parts[l] = jnp.stack([up.reshape(n_z, n_x, n_yh * run, ff), down])
        riders = None
        if l == 0:
            loss_tile = jnp.full((1, 8, quarter // 8), loss_sum)
            gains = jnp.stack(gain_rows).reshape(SECTIONS, 8, quarter // 8)
            riders = [jnp.concatenate([gains, loss_tile], 0)]
            riders += added("yh") + added("z") + added("x")
            riders.append(lambda v: (group_exchange(v[:SECTIONS], me), v[SECTIONS, 0, 0]))
        if l in X_FIRST:
            part, z_done = ring_scatter(parts[l], "z", 1, 0, z_done, riders)
            small[l] = part.astype(bf16)
        else:
            part, x_done = ring_scatter(parts[l], "x", 2, 0, x_done)
            small[l] = part.astype(bf16)

    small_z = jnp.stack([small[l] for l in late])
    small_z, _ = ring_scatter(small_z, "z", 2, 1, (), riders)
    small_x, _ = ring_scatter(jnp.stack([small[l] for l in X_FIRST]), "x", 2, 1)
    summed = [
        small_x[X_FIRST.index(l)] if l in X_FIRST else small_z[late.index(l)]
        for l in range(SECTIONS)
    ]
    summed = jnp.stack(summed)
    ups = summed[:, 0].reshape(SECTIONS, n_yh, run, ff)
    downs = summed[:, 1].reshape(SECTIONS, 2, n_yh, ff_rows, ff).transpose(0, 2, 1, 3, 4)
    both = jnp.concatenate([ups, downs.reshape(SECTIONS, n_yh, run, ff)], 2)
    low, high = both[:, 0], both[:, 1]
    keep, send = jnp.where(is_low, low, high), jnp.where(is_low, high, low).astype(bf16)
    both = (keep + swap(send, "yh", 1).astype(f32)).astype(bf16)
    both = group_exchange(both, me)
    gains, loss_total = riders[0]
    gain_total = gains.reshape(SECTIONS, width // (run * SECTIONS), run)
    gain_total = gain_total.transpose(1, 0, 2).reshape(width) / norm_gain[0]
    grad_up = both[:, :run].reshape(SECTIONS * run, ff).astype(f32) * gain_col
    down = both[:, run:].reshape(SECTIONS, 2, ff_rows, n_z // 2, span).transpose(2, 1, 3, 0, 4)
    down = down.reshape(ff_rows * n_z, SECTIONS * span)
    grad_down = matmul(down, deal, ((1,), (1,))).reshape(ff_rows, width)
    return (grad_up[None], grad_down[None], gain_total[None], loss_total)


def solution(mesh):
    sizes = (2, 2, mesh.shape["dp"] // 8, 4, 2)
    fine = Mesh(mesh.devices.reshape(sizes), ("yl", "core", "z", "x", "yh"))
    section, dp = ("yl", "core"), ("z", "x", "yh")
    return jax.shard_map(
        on_device,
        mesh=fine,
        in_specs=(
            P(dp, None),
            P(dp),
            P(dp, None),
            P(dp),
            P(),
            P(section, None),
            P(section, dp, None),
            P(section, dp, None),
        ),
        out_specs=(P(section, dp, None), P(section, dp, None), P(section, None), P()),
        check_vma=False,
    )
```
